32 devices in a mesh: interval: 4 (over y, x), slab: 8 (over z, core).
Axes of the slice: x: 2, y: 2, z: 4, core: 2. Of those that a mesh axis runs over, the one named last changes fastest.
Arguments:
- states: float32 [8, 16, 256, 512], P('interval', 'slab'), may hold values from -0.9 to 0.9
- occupations: int32 [8], P('interval'), may hold values from 1 to 64
- core_density: float32 [16, 256, 512], P('slab'), may hold values from 0.1 to 1
Outputs:
- potential: float32 [16, 256, 512], P('slab', 'interval')
The draws below stay inside these ranges and needn't reach their ends.
All inputs are finite; a program needn't handle non-finite values.
Results may differ from the reference program's by a relative error of at most 0.00002.
Values sent between devices are 32-bit elements; how exact they have to be, the bound alone decides.
A program may use at most 64 MiB of HBM per device.

```python
import math
import jax
import jax.numpy as jnp
from jax import lax

NX = 256
NY = 512
NZ = 16
NSTATES = 8


def set_ends(array, stream_key, smallest, top_value):
    index_at = [jax.random.randint(jax.random.fold_in(stream_key, axis), (), 0, length) for axis, length in enumerate(array.shape)]
    longest = array.shape.index(max(array.shape))
    neighbour = index_at[:longest] + [(index_at[longest] + 1) % array.shape[longest]] + index_at[longest + 1:]
    return array.at[tuple(index_at)].set(smallest).at[tuple(neighbour)].set(top_value)


def levels(stream_key, shape, split, smallest, high):
    def one(dim, parts):
        draws = jax.random.uniform(jax.random.fold_in(jax.random.fold_in(stream_key, 6), dim), (parts,), jnp.float32, smallest / len(split), high / len(split))
        return jnp.repeat(jnp.exp(draws), shape[dim] // parts).reshape((-1,) + (1,) * (len(shape) - dim - 1))

    loudness = one(*split[0])
    for cut in split[1:]:
        loudness = loudness * one(*cut)
    return loudness


def normal_values(stream_key, dims, deviation, reach, cuts=(), kind=jnp.bfloat16):
    values = deviation * jax.random.normal(stream_key, dims, jnp.float32)
    if cuts:
        values = values * levels(stream_key, dims, cuts, -0.22, 0.18)
    return jnp.clip(values, -reach, reach).astype(kind)


def setup_inputs(seed: int = 0) -> dict:
    seeds = jax.random.split(jax.random.key(seed), 4)
    states = normal_values(seeds[0], (NSTATES, NZ, NX, NY), 0.15, 0.9, ((0, 4), (1, 8)), jnp.float32)
    occupations = set_ends(jax.random.randint(seeds[1], (NSTATES,), 1, 65), jax.random.fold_in(seeds[1], 1), 1, 64).astype(jnp.int32)
    core_density = jnp.clip(jnp.exp(math.log(1.0) - 2.3025851 * jax.random.uniform(seeds[2], (NZ, NX, NY), jnp.float32) ** levels(seeds[2], (NZ, NX, NY), ((0, 8),), -0.2, 0.2)), 0.1, 1.0)
    return {"states": states, "occupations": occupations, "core_density": core_density}


spacing = 0.25
denominator = 64.0
pbe_kappa = 0.804
pbe_mu = 0.2195149727645171
pbe_beta = 0.06672455060314922
pw_alpha = 0.0310907

def deriv_roll(field, axis):
    near = jnp.roll(field, -1, axis) - jnp.roll(field, 1, axis)
    far = jnp.roll(field, -2, axis) - jnp.roll(field, 2, axis)
    return (8.0 * near - far) / (12.0 * spacing)

def pbe_energy(density, grad_sq):
    pbe_gamma = (1.0 - jnp.log(2.0)) / jnp.pi ** 2
    k_fermi = jnp.cbrt(3.0 * jnp.pi ** 2 * density)
    ex_unif = -0.75 * jnp.cbrt(3.0 / jnp.pi) * jnp.cbrt(density)
    s_sq = grad_sq / (4.0 * k_fermi ** 2 * density ** 2)
    f_exch = 1.0 + pbe_kappa - pbe_kappa / (1.0 + pbe_mu * s_sq / pbe_kappa)
    radius = jnp.cbrt(3.0 / (4.0 * jnp.pi * density))
    root_r = jnp.sqrt(radius)
    lower = 2.0 * pw_alpha * (7.5957 * root_r + 3.5876 * radius + 1.6382 * radius * root_r + 0.49294 * radius ** 2)
    e_corr = -2.0 * pw_alpha * (1.0 + 0.2137 * radius) * jnp.log(1.0 + 1.0 / lower)
    k_screen = jnp.sqrt(4.0 * k_fermi / jnp.pi)
    t_sq = grad_sq / (4.0 * k_screen ** 2 * density ** 2)
    factor = pbe_beta / pbe_gamma / jnp.expm1(-e_corr / pbe_gamma)
    ratio_t = (1.0 + factor * t_sq) / (1.0 + factor * t_sq + factor ** 2 * t_sq ** 2)
    h_term = pbe_gamma * jnp.log(1.0 + pbe_beta / pbe_gamma * t_sq * ratio_t)
    return density * (ex_unif * f_exch + e_corr + h_term)

def local_derivs(density, grad_sq):
    return jax.grad(lambda rho, grd: jnp.sum(pbe_energy(rho, grd)), argnums=(0, 1))(density, grad_sq)

def reference(states, occupations, core_density):
    weights = occupations.astype(jnp.float32) / denominator

    def accumulate(index, total):
        one_state = lax.dynamic_index_in_dim(states, index, 0, keepdims=False)
        return total + weights[index] * one_state * one_state
    valence = lax.fori_loop(0, states.shape[0], accumulate, jnp.zeros(states.shape[1:], jnp.float32))
    density = valence + core_density
    grad_z = deriv_roll(density, 0)
    grad_x = deriv_roll(density, 1)
    grad_y = deriv_roll(density, 2)
    grad_sq = grad_z * grad_z + grad_x * grad_x + grad_y * grad_y
    energy_rho, energy_grad = local_derivs(density, grad_sq)
    diverge = deriv_roll(2.0 * energy_grad * grad_z, 0) + deriv_roll(2.0 * energy_grad * grad_x, 1) + deriv_roll(2.0 * energy_grad * grad_y, 2)
    return energy_rho - diverge
```

```python
import functools
import math

import jax
import jax.numpy as jnp
from jax import lax
from jax.experimental import pallas as pl
from jax.experimental.pallas import tpu as pltpu
from jax.sharding import PartitionSpec as P

spacing = 0.25
denominator = 64.0
pbe_kappa = 0.804
pbe_mu = 0.2195149727645171
pbe_beta = 0.06672455060314922
pw_alpha = 0.0310907
pbe_gamma = (1.0 - math.log(2.0)) / math.pi**2
MESH = pl.DeviceIdType.MESH
edge = 8


def five_point(low2, low1, high1, high2):
    return (8.0 * (high1 - low1) - (high2 - low2)) * (1.0 / (12.0 * spacing))


def deriv_y(field):
    axis = field.ndim - 1
    count = field.shape[axis]
    return five_point(
        pltpu.roll(field, 2, axis),
        pltpu.roll(field, 1, axis),
        pltpu.roll(field, count - 1, axis),
        pltpu.roll(field, count - 2, axis),
    )


def deriv_x(tall):
    return five_point(
        tall[:, edge - 2 : -edge - 2],
        tall[:, edge - 1 : -edge - 1],
        tall[:, edge + 1 : 1 - edge],
        tall[:, edge + 2 : 2 - edge],
    )


def deriv_z(tall):
    count = tall.shape[0] - 4
    return five_point(
        tall[:count], tall[1 : count + 1], tall[3 : count + 3], tall[4 : count + 4]
    )


def pbe_derivs(n, g):
    k_one = (3.0 * math.pi**2) ** (1.0 / 3.0)
    ex_one = -0.75 * (3.0 / math.pi) ** (1.0 / 3.0)
    r_one = (3.0 / (4.0 * math.pi)) ** (1.0 / 3.0)
    s_one = 1.0 / (4.0 * k_one**2)
    t_one = math.pi / (16.0 * k_one)
    ratio = pbe_beta / pbe_gamma
    inv_six = jnp.exp(jnp.log(n) * (-1.0 / 6.0))
    inv = inv_six * inv_six
    inv2 = inv * inv
    inv4 = inv2 * inv2
    cube = n * inv2
    s_sq = (s_one * g) * (inv4 * inv4)
    u_inv = 1.0 / (1.0 + (pbe_mu / pbe_kappa) * s_sq)
    f_exch = (1.0 + pbe_kappa) - pbe_kappa * u_inv
    f_slope = pbe_mu * u_inv * u_inv
    ex_rho = (ex_one * cube) * ((4.0 / 3.0) * f_exch - (8.0 / 3.0) * f_slope * s_sq)

    radius = r_one * inv
    root = math.sqrt(r_one) * inv_six
    two_a = 2.0 * pw_alpha
    lower = (two_a * root) * (
        7.5957 + root * (3.5876 + root * (1.6382 + root * 0.49294))
    )
    slope = (two_a * root) * (
        0.5 * 7.5957 + root * (3.5876 + root * (1.5 * 1.6382 + root * (2.0 * 0.49294)))
    )
    pair_inv = 1.0 / (lower * (lower + 1.0))
    log_term = jnp.log(1.0 + (lower + 1.0) * pair_inv)
    front = two_a + (two_a * 0.2137) * radius
    e_corr = -front * log_term
    n_ec = (1.0 / 3.0) * ((two_a * 0.2137) * radius * log_term - front * slope * pair_inv)

    grown = jnp.exp(e_corr * (-1.0 / pbe_gamma))
    factor = ratio / (grown - 1.0)
    t_sq = (t_one * g) * (inv4 * inv2 * inv)
    y = factor * t_sq
    lift = 1.0 + y
    den = lift + y * y
    add = (ratio * t_sq) * lift
    full = den + add
    inv_full = 1.0 / (den * full)
    h_term = pbe_gamma * jnp.log(1.0 + add * (full * inv_full))
    h_t = (pbe_beta * inv_full) * (1.0 + 2.0 * y)
    h_ec = -(y * y) * (y * (2.0 + y)) * inv_full * grown
    e_rho = ex_rho + e_corr + h_term + n_ec + h_ec * n_ec - (7.0 / 3.0) * (t_sq * h_t)
    e_grad = inv4 * (t_one * h_t + (ex_one * s_one) * f_slope)
    return e_rho, e_grad


def kernel(
    peers, slabs, rows,
    states, occ, core, out,
    stage, core_v, snd, rcv, dens, fz, fx,
    in_sem, core_sem, rs_send, rs_recv, z_send, z_recv, x_send, x_recv,
):
    nst, nz, wide = stage.shape[1], stage.shape[2], stage.shape[3]
    chunks = wide // rows
    me = lax.axis_index("interval")
    sl = lax.axis_index("slab")
    z_low = lax.rem(sl + slabs - 1, slabs)
    z_high = lax.rem(sl + 1, slabs)
    x_low = lax.rem(me + peers - 1, peers)
    x_high = lax.rem(me + 1, peers)
    order = [0] + ([chunks - 1] if chunks > 1 else []) + list(range(1, chunks - 1))

    def pull(k, c):
        start = pl.multiple_of(lax.rem(me + k, peers) * wide + c * rows, 8)
        return pltpu.make_async_copy(
            states.at[:, :, pl.ds(start, rows), :],
            stage.at[k, :, :, pl.ds(c * rows, rows), :],
            in_sem.at[k, c],
        )

    for c in order:
        for k in [*range(1, peers), 0]:
            pull(k, c).start()
    core_copy = pltpu.make_async_copy(
        core.at[:, pl.ds(pl.multiple_of(me * wide, 8), wide), :], core_v, core_sem
    )
    core_copy.start()

    barrier = pltpu.get_barrier_semaphore()
    for k in range(1, peers):
        pl.semaphore_signal(
            barrier, inc=1, device_id=(lax.rem(me + k, peers), sl), device_id_type=MESH
        )
    for z in (z_low, z_high):
        pl.semaphore_signal(barrier, inc=1, device_id=(me, z), device_id_type=MESH)

    weights = [occ[s].astype(jnp.float32) * (1.0 / denominator) for s in range(nst)]

    def term(k, at):
        total = None
        for s in range(nst):
            value = stage[k, s, :, pl.ds(at, edge), :]
            part = (weights[s] * value) * value
            total = part if total is None else total + part
        return total

    def tiles(c, body):
        def step(t, _):
            body(pl.multiple_of(c * rows + t * edge, edge))
            return 0

        lax.fori_loop(0, rows // edge, step, 0)

    def share(k, c):
        span = pl.ds(c * rows, rows)
        return pltpu.make_async_remote_copy(
            src_ref=snd.at[k - 1, :, span, :],
            dst_ref=rcv.at[k - 1, :, span, :],
            send_sem=rs_send.at[k - 1, c],
            recv_sem=rs_recv.at[k - 1, c],
            device_id=(lax.rem(me + k, peers), sl),
            device_id_type=MESH,
        )

    def planes(field, way, c):
        ref = (dens, fz)[field]
        pad = (edge, 0)[field]
        span = pl.ds(pad + c * rows, rows)
        source, target = ((2, nz + 2), (nz, 0))[way]
        return pltpu.make_async_remote_copy(
            src_ref=ref.at[pl.ds(source, 2), span, :],
            dst_ref=ref.at[pl.ds(target, 2), span, :],
            send_sem=z_send.at[field, way, c],
            recv_sem=z_recv.at[field, way, c],
            device_id=(me, (z_low, z_high)[way]),
            device_id_type=MESH,
        )

    def sides(field, way):
        ref = (dens.at[pl.ds(2, nz)], fx)[field]
        source, target = ((edge, edge + wide), (wide, 0))[way]
        return pltpu.make_async_remote_copy(
            src_ref=ref.at[:, pl.ds(source, edge), :],
            dst_ref=ref.at[:, pl.ds(target, edge), :],
            send_sem=x_send.at[field, way],
            recv_sem=x_recv.at[field, way],
            device_id=((x_low, x_high)[way], sl),
            device_id_type=MESH,
        )

    started = []

    def start(copy):
        copy.start()
        started.append(copy)

    first = True
    for c in order:
        for k in range(1, peers):
            pull(k, c).wait()

            def fill(at, k=k):
                snd[k - 1, :, pl.ds(at, edge), :] = term(k, at)

            tiles(c, fill)
            if first:
                pl.semaphore_wait(barrier, peers + 1)
                first = False
            start(share(k, c))
    core_copy.wait()

    def gather(c):
        pull(0, c).wait()
        for k in range(1, peers):
            share(k, c).wait_recv()

        def add(at):
            total = term(0, at)
            for k in range(1, peers):
                total = total + rcv[k - 1, :, pl.ds(at, edge), :]
            dens[2 : nz + 2, pl.ds(at + edge, edge), :] = (
                total + core_v[:, pl.ds(at, edge), :]
            )

        tiles(c, add)
        if c == 0:
            start(sides(0, 0))
        if c == chunks - 1:
            start(sides(0, 1))
        for way in (0, 1):
            start(planes(0, way, c))

    def energy(c):
        for way in (0, 1):
            planes(0, way, c).wait_recv()
        if c == chunks - 1:
            sides(0, 0).wait_recv()
        if c == 0:
            sides(0, 1).wait_recv()

        def work(at):
            inner = pl.ds(at + edge, edge)
            n = dens[2 : nz + 2, inner, :]
            grad_z = deriv_z(dens[:, inner, :])
            grad_x = deriv_x(dens[2 : nz + 2, pl.ds(at, 3 * edge), :])
            grad_y = deriv_y(n)
            g = grad_z * grad_z + grad_x * grad_x + grad_y * grad_y
            e_rho, e_grad = pbe_derivs(n, g)
            twice = 2.0 * e_grad
            fz[2 : nz + 2, pl.ds(at, edge), :] = twice * grad_z
            fx[:, inner, :] = twice * grad_x
            out[:, pl.ds(at, edge), :] = e_rho - deriv_y(twice * grad_y)

        tiles(c, work)
        if c == 0:
            start(sides(1, 0))
        if c == chunks - 1:
            start(sides(1, 1))
        for way in (0, 1):
            start(planes(1, way, c))

    def diverge(c):
        for way in (0, 1):
            planes(1, way, c).wait_recv()
        if c == chunks - 1:
            sides(1, 0).wait_recv()
        if c == 0:
            sides(1, 1).wait_recv()

        def work(at):
            span = pl.ds(at, edge)
            out[:, span, :] = out[:, span, :] - (
                deriv_z(fz[:, span, :]) + deriv_x(fx[:, pl.ds(at, 3 * edge), :])
            )

        tiles(c, work)

    gathered, done = set(), set()
    for c in order:
        gather(c)
        gathered.add(c)
        for d in order:
            near = {e for e in (d - 1, d, d + 1) if 0 <= e < chunks}
            ends = d not in (0, chunks - 1) or {0, chunks - 1} <= gathered
            if d not in done and near <= gathered and ends and len(gathered) > 2:
                energy(d)
                done.add(d)
                break
    for d in order:
        if d not in done:
            energy(d)
    for d in order:
        diverge(d)
    for copy in started:
        copy.wait_send()


def shards(peers, slabs, states, occupations, core_density):
    nst, nz, full, deep = states.shape
    wide = full // peers
    rows = 16 if wide % 16 == 0 else 8
    chunks = wide // rows
    f32 = jnp.float32
    dma = pltpu.SemaphoreType.DMA
    return pl.pallas_call(
        functools.partial(kernel, peers, slabs, rows),
        out_shape=jax.ShapeDtypeStruct((nz, wide, deep), f32),
        in_specs=[
            pl.BlockSpec(memory_space=pl.ANY),
            pl.BlockSpec(memory_space=pltpu.SMEM),
            pl.BlockSpec(memory_space=pl.ANY),
        ],
        out_specs=pl.BlockSpec(memory_space=pltpu.VMEM),
        scratch_shapes=[
            pltpu.VMEM((peers, nst, nz, wide, deep), f32),
            pltpu.VMEM((nz, wide, deep), f32),
            pltpu.VMEM((peers - 1, nz, wide, deep), f32),
            pltpu.VMEM((peers - 1, nz, wide, deep), f32),
            pltpu.VMEM((nz + 4, wide + 2 * edge, deep), f32),
            pltpu.VMEM((nz + 4, wide, deep), f32),
            pltpu.VMEM((nz, wide + 2 * edge, deep), f32),
            dma((peers, chunks)),
            dma,
            dma((peers - 1, chunks)),
            dma((peers - 1, chunks)),
            dma((2, 2, chunks)),
            dma((2, 2, chunks)),
            dma((2, 2)),
            dma((2, 2)),
        ],
        compiler_params=pltpu.CompilerParams(
            collective_id=0, has_side_effects=True, vmem_limit_bytes=48 * 1024 * 1024
        ),
    )(states, occupations, core_density)


def solution(mesh):
    return jax.shard_map(
        functools.partial(shards, mesh.shape["interval"], mesh.shape["slab"]),
        mesh=mesh,
        in_specs=(P("interval", "slab", None, None), P("interval"), P("slab", None, None)),
        out_specs=P("slab", "interval", None),
        check_vma=False,
    )
```

```python
import functools
import math

import jax
import jax.numpy as jnp
from jax import lax
from jax.experimental import pallas as pl
from jax.experimental.pallas import tpu as pltpu
from jax.sharding import PartitionSpec as P

spacing = 0.25
denominator = 64.0
pbe_kappa = 0.804
pbe_mu = 0.2195149727645171
pbe_beta = 0.06672455060314922
pw_alpha = 0.0310907
pbe_gamma = (1.0 - math.log(2.0)) / math.pi**2
MESH = pl.DeviceIdType.MESH
edge = 8


def five_point(low2, low1, high1, high2):
    return (8.0 * (high1 - low1) - (high2 - low2)) * (1.0 / (12.0 * spacing))


def deriv_y(field):
    axis = field.ndim - 1
    count = field.shape[axis]
    return five_point(
        pltpu.roll(field, 2, axis),
        pltpu.roll(field, 1, axis),
        pltpu.roll(field, count - 1, axis),
        pltpu.roll(field, count - 2, axis),
    )


def deriv_x(tall):
    return five_point(
        tall[:, edge - 2 : -edge - 2],
        tall[:, edge - 1 : -edge - 1],
        tall[:, edge + 1 : 1 - edge],
        tall[:, edge + 2 : 2 - edge],
    )


def deriv_z(tall):
    count = tall.shape[0] - 4
    return five_point(
        tall[:count], tall[1 : count + 1], tall[3 : count + 3], tall[4 : count + 4]
    )


def pbe_derivs(n, g):
    k_one = (3.0 * math.pi**2) ** (1.0 / 3.0)
    ex_one = -0.75 * (3.0 / math.pi) ** (1.0 / 3.0)
    r_one = (3.0 / (4.0 * math.pi)) ** (1.0 / 3.0)
    s_one = 1.0 / (4.0 * k_one**2)
    t_one = math.pi / (16.0 * k_one)
    ratio = pbe_beta / pbe_gamma
    inv_six = jnp.exp(jnp.log(n) * (-1.0 / 6.0))
    inv = inv_six * inv_six
    inv2 = inv * inv
    inv4 = inv2 * inv2
    cube = n * inv2
    s_sq = (s_one * g) * (inv4 * inv4)
    u_inv = 1.0 / (1.0 + (pbe_mu / pbe_kappa) * s_sq)
    f_exch = (1.0 + pbe_kappa) - pbe_kappa * u_inv
    f_slope = pbe_mu * u_inv * u_inv
    ex_rho = (ex_one * cube) * ((4.0 / 3.0) * f_exch - (8.0 / 3.0) * f_slope * s_sq)

    radius = r_one * inv
    root = math.sqrt(r_one) * inv_six
    two_a = 2.0 * pw_alpha
    lower = (two_a * root) * (
        7.5957 + root * (3.5876 + root * (1.6382 + root * 0.49294))
    )
    slope = (two_a * root) * (
        0.5 * 7.5957 + root * (3.5876 + root * (1.5 * 1.6382 + root * (2.0 * 0.49294)))
    )
    pair_inv = 1.0 / (lower * (lower + 1.0))
    log_term = jnp.log(1.0 + (lower + 1.0) * pair_inv)
    front = two_a + (two_a * 0.2137) * radius
    e_corr = -front * log_term
    n_ec = (1.0 / 3.0) * ((two_a * 0.2137) * radius * log_term - front * slope * pair_inv)

    grown = jnp.exp(e_corr * (-1.0 / pbe_gamma))
    factor = ratio / (grown - 1.0)
    t_sq = (t_one * g) * (inv4 * inv2 * inv)
    y = factor * t_sq
    lift = 1.0 + y
    den = lift + y * y
    add = (ratio * t_sq) * lift
    full = den + add
    inv_full = 1.0 / (den * full)
    h_term = pbe_gamma * jnp.log(1.0 + add * (full * inv_full))
    h_t = (pbe_beta * inv_full) * (1.0 + 2.0 * y)
    h_ec = -(y * y) * (y * (2.0 + y)) * inv_full * grown
    e_rho = ex_rho + e_corr + h_term + n_ec + h_ec * n_ec - (7.0 / 3.0) * (t_sq * h_t)
    e_grad = inv4 * (t_one * h_t + (ex_one * s_one) * f_slope)
    return e_rho, e_grad


def kernel(
    peers, slabs, rows,
    states, occ, core, out,
    stage, core_v, snd, rcv, dens, fz, fx,
    in_sem, core_sem, rs_send, rs_recv, z_send, z_recv, x_send, x_recv,
):
    nst, nz, wide = stage.shape[1], stage.shape[2], stage.shape[3]
    chunks = wide // rows
    me = lax.axis_index("interval")
    sl = lax.axis_index("slab")
    z_low = lax.rem(sl + slabs - 1, slabs)
    z_high = lax.rem(sl + 1, slabs)
    x_low = lax.rem(me + peers - 1, peers)
    x_high = lax.rem(me + 1, peers)
    order = [0] + ([chunks - 1] if chunks > 1 else []) + list(range(1, chunks - 1))

    def pull(k, c):
        start = pl.multiple_of(lax.rem(me + k, peers) * wide + c * rows, 8)
        return pltpu.make_async_copy(
            states.at[:, :, pl.ds(start, rows), :],
            stage.at[k, :, :, pl.ds(c * rows, rows), :],
            in_sem.at[k, c],
        )

    for c in order:
        for k in [*range(1, peers), 0]:
            pull(k, c).start()
    core_copy = pltpu.make_async_copy(
        core.at[:, pl.ds(pl.multiple_of(me * wide, 8), wide), :], core_v, core_sem
    )
    core_copy.start()

    barrier = pltpu.get_barrier_semaphore()
    for k in range(1, peers):
        pl.semaphore_signal(
            barrier, inc=1, device_id=(lax.rem(me + k, peers), sl), device_id_type=MESH
        )
    for z in (z_low, z_high):
        pl.semaphore_signal(barrier, inc=1, device_id=(me, z), device_id_type=MESH)

    weights = [occ[s].astype(jnp.float32) * (1.0 / denominator) for s in range(nst)]

    def term(k, at):
        total = None
        for s in range(nst):
            value = stage[k, s, :, pl.ds(at, edge), :]
            part = (weights[s] * value) * value
            total = part if total is None else total + part
        return total

    def tiles(c, body):
        def step(t, _):
            body(pl.multiple_of(c * rows + t * edge, edge))
            return 0

        lax.fori_loop(0, rows // edge, step, 0)

    def share(k, c):
        span = pl.ds(c * rows, rows)
        return pltpu.make_async_remote_copy(
            src_ref=snd.at[k - 1, :, span, :],
            dst_ref=rcv.at[k - 1, :, span, :],
            send_sem=rs_send.at[k - 1, c],
            recv_sem=rs_recv.at[k - 1, c],
            device_id=(lax.rem(me + k, peers), sl),
            device_id_type=MESH,
        )

    def planes(field, way, c):
        ref = (dens, fz)[field]
        pad = (edge, 0)[field]
        span = pl.ds(pad + c * rows, rows)
        source, target = ((2, nz + 2), (nz, 0))[way]
        return pltpu.make_async_remote_copy(
            src_ref=ref.at[pl.ds(source, 2), span, :],
            dst_ref=ref.at[pl.ds(target, 2), span, :],
            send_sem=z_send.at[field, way, c],
            recv_sem=z_recv.at[field, way, c],
            device_id=(me, (z_low, z_high)[way]),
            device_id_type=MESH,
        )

    def sides(field, way):
        ref = (dens.at[pl.ds(2, nz)], fx)[field]
        source, target = ((edge, edge + wide), (wide, 0))[way]
        return pltpu.make_async_remote_copy(
            src_ref=ref.at[:, pl.ds(source, edge), :],
            dst_ref=ref.at[:, pl.ds(target, edge), :],
            send_sem=x_send.at[field, way],
            recv_sem=x_recv.at[field, way],
            device_id=((x_low, x_high)[way], sl),
            device_id_type=MESH,
        )

    started = []

    def start(copy):
        copy.start()
        started.append(copy)

    first = True
    for c in order:
        for k in range(1, peers):
            pull(k, c).wait()

            def fill(at, k=k):
                snd[k - 1, :, pl.ds(at, edge), :] = term(k, at)

            tiles(c, fill)
            if first:
                pl.semaphore_wait(barrier, peers + 1)
                first = False
            start(share(k, c))
    core_copy.wait()

    def gather(c):
        pull(0, c).wait()
        for k in range(1, peers):
            share(k, c).wait_recv()

        def add(at):
            total = term(0, at)
            for k in range(1, peers):
                total = total + rcv[k - 1, :, pl.ds(at, edge), :]
            dens[2 : nz + 2, pl.ds(at + edge, edge), :] = (
                total + core_v[:, pl.ds(at, edge), :]
            )

        tiles(c, add)
        if c == 0:
            start(sides(0, 0))
        if c == chunks - 1:
            start(sides(0, 1))
        for way in (0, 1):
            start(planes(0, way, c))

    def energy(c):
        for way in (0, 1):
            planes(0, way, c).wait_recv()
        if c == chunks - 1:
            sides(0, 0).wait_recv()
        if c == 0:
            sides(0, 1).wait_recv()

        def work(at):
            inner = pl.ds(at + edge, edge)
            n = dens[2 : nz + 2, inner, :]
            grad_z = deriv_z(dens[:, inner, :])
            grad_x = deriv_x(dens[2 : nz + 2, pl.ds(at, 3 * edge), :])
            grad_y = deriv_y(n)
            g = grad_z * grad_z + grad_x * grad_x + grad_y * grad_y
            e_rho, e_grad = pbe_derivs(n, g)
            twice = 2.0 * e_grad
            fz[2 : nz + 2, pl.ds(at, edge), :] = twice * grad_z
            fx[:, inner, :] = twice * grad_x
            out[:, pl.ds(at, edge), :] = e_rho - deriv_y(twice * grad_y)

        tiles(c, work)
        if c == 0:
            start(sides(1, 0))
        if c == chunks - 1:
            start(sides(1, 1))
        for way in (0, 1):
            start(planes(1, way, c))

    def diverge(c):
        for way in (0, 1):
            planes(1, way, c).wait_recv()
        if c == chunks - 1:
            sides(1, 0).wait_recv()
        if c == 0:
            sides(1, 1).wait_recv()

        def work(at):
            span = pl.ds(at, edge)
            out[:, span, :] = out[:, span, :] - (
                deriv_z(fz[:, span, :]) + deriv_x(fx[:, pl.ds(at, 3 * edge), :])
            )

        tiles(c, work)

    gathered, done = set(), set()
    for c in order:
        gather(c)
        gathered.add(c)
        for d in order:
            near = {e for e in (d - 1, d, d + 1) if 0 <= e < chunks}
            ends = d not in (0, chunks - 1) or {0, chunks - 1} <= gathered
            if d not in done and near <= gathered and ends and len(gathered) > 2:
                energy(d)
                done.add(d)
                break
    for d in order:
        if d not in done:
            energy(d)
    for d in order:
        diverge(d)
    for copy in started:
        copy.wait_send()


def shards(peers, slabs, states, occupations, core_density):
    nst, nz, full, deep = states.shape
    wide = full // peers
    rows = edge
    chunks = wide // rows
    f32 = jnp.float32
    dma = pltpu.SemaphoreType.DMA
    return pl.pallas_call(
        functools.partial(kernel, peers, slabs, rows),
        out_shape=jax.ShapeDtypeStruct((nz, wide, deep), f32),
        in_specs=[
            pl.BlockSpec(memory_space=pl.ANY),
            pl.BlockSpec(memory_space=pltpu.SMEM),
            pl.BlockSpec(memory_space=pl.ANY),
        ],
        out_specs=pl.BlockSpec(memory_space=pltpu.VMEM),
        scratch_shapes=[
            pltpu.VMEM((peers, nst, nz, wide, deep), f32),
            pltpu.VMEM((nz, wide, deep), f32),
            pltpu.VMEM((peers - 1, nz, wide, deep), f32),
            pltpu.VMEM((peers - 1, nz, wide, deep), f32),
            pltpu.VMEM((nz + 4, wide + 2 * edge, deep), f32),
            pltpu.VMEM((nz + 4, wide, deep), f32),
            pltpu.VMEM((nz, wide + 2 * edge, deep), f32),
            dma((peers, chunks)),
            dma,
            dma((peers - 1, chunks)),
            dma((peers - 1, chunks)),
            dma((2, 2, chunks)),
            dma((2, 2, chunks)),
            dma((2, 2)),
            dma((2, 2)),
        ],
        compiler_params=pltpu.CompilerParams(
            collective_id=0, has_side_effects=True, vmem_limit_bytes=67043328
        ),
    )(states, occupations, core_density)


def solution(mesh):
    return jax.shard_map(
        functools.partial(shards, mesh.shape["interval"], mesh.shape["slab"]),
        mesh=mesh,
        in_specs=(P("interval", "slab", None, None), P("interval"), P("slab", None, None)),
        out_specs=P("slab", "interval", None),
        check_vma=False,
    )
```

```python
import functools
import math

import jax
import jax.numpy as jnp
from jax import lax
from jax.experimental import pallas as pl
from jax.experimental.pallas import tpu as pltpu
from jax.sharding import PartitionSpec as P

spacing = 0.25
denominator = 64.0
pbe_kappa = 0.804
pbe_mu = 0.2195149727645171
pbe_beta = 0.06672455060314922
pw_alpha = 0.0310907
pbe_gamma = (1.0 - math.log(2.0)) / math.pi**2
MESH = pl.DeviceIdType.MESH
edge = 8


def five_point(low2, low1, high1, high2):
    return (8.0 * (high1 - low1) - (high2 - low2)) * (1.0 / (12.0 * spacing))


def deriv_y(field):
    axis = field.ndim - 1
    count = field.shape[axis]
    return five_point(
        pltpu.roll(field, 2, axis),
        pltpu.roll(field, 1, axis),
        pltpu.roll(field, count - 1, axis),
        pltpu.roll(field, count - 2, axis),
    )


def deriv_x(tall):
    return five_point(
        tall[:, edge - 2 : -edge - 2],
        tall[:, edge - 1 : -edge - 1],
        tall[:, edge + 1 : 1 - edge],
        tall[:, edge + 2 : 2 - edge],
    )


def deriv_z(tall):
    count = tall.shape[0] - 4
    return five_point(
        tall[:count], tall[1 : count + 1], tall[3 : count + 3], tall[4 : count + 4]
    )


def pbe_derivs(n, g):
    k_one = (3.0 * math.pi**2) ** (1.0 / 3.0)
    ex_one = -0.75 * (3.0 / math.pi) ** (1.0 / 3.0)
    r_one = (3.0 / (4.0 * math.pi)) ** (1.0 / 3.0)
    s_one = 1.0 / (4.0 * k_one**2)
    t_one = math.pi / (16.0 * k_one)
    ratio = pbe_beta / pbe_gamma
    inv_six = jnp.exp(jnp.log(n) * (-1.0 / 6.0))
    inv = inv_six * inv_six
    inv2 = inv * inv
    inv4 = inv2 * inv2
    cube = n * inv2
    s_sq = (s_one * g) * (inv4 * inv4)
    u_inv = 1.0 / (1.0 + (pbe_mu / pbe_kappa) * s_sq)
    f_exch = (1.0 + pbe_kappa) - pbe_kappa * u_inv
    f_slope = pbe_mu * u_inv * u_inv
    ex_rho = (ex_one * cube) * ((4.0 / 3.0) * f_exch - (8.0 / 3.0) * f_slope * s_sq)

    radius = r_one * inv
    root = math.sqrt(r_one) * inv_six
    two_a = 2.0 * pw_alpha
    lower = (two_a * root) * (
        7.5957 + root * (3.5876 + root * (1.6382 + root * 0.49294))
    )
    slope = (two_a * root) * (
        0.5 * 7.5957 + root * (3.5876 + root * (1.5 * 1.6382 + root * (2.0 * 0.49294)))
    )
    pair_inv = 1.0 / (lower * (lower + 1.0))
    log_term = jnp.log(1.0 + (lower + 1.0) * pair_inv)
    front = two_a + (two_a * 0.2137) * radius
    e_corr = -front * log_term
    n_ec = (1.0 / 3.0) * ((two_a * 0.2137) * radius * log_term - front * slope * pair_inv)

    grown = jnp.exp(e_corr * (-1.0 / pbe_gamma))
    factor = ratio / (grown - 1.0)
    t_sq = (t_one * g) * (inv4 * inv2 * inv)
    y = factor * t_sq
    lift = 1.0 + y
    den = lift + y * y
    add = (ratio * t_sq) * lift
    full = den + add
    inv_full = 1.0 / (den * full)
    h_term = pbe_gamma * jnp.log(1.0 + add * (full * inv_full))
    h_t = (pbe_beta * inv_full) * (1.0 + 2.0 * y)
    h_ec = -(y * y) * (y * (2.0 + y)) * inv_full * grown
    e_rho = ex_rho + e_corr + h_term + n_ec + h_ec * n_ec - (7.0 / 3.0) * (t_sq * h_t)
    e_grad = inv4 * (t_one * h_t + (ex_one * s_one) * f_slope)
    return e_rho, e_grad


def kernel(
    peers, slabs, rows,
    states, occ, core, out,
    stage, core_v, snd, rcv, dens, fz, fx,
    in_sem, core_sem, rs_send, rs_recv, z_send, z_recv, x_send, x_recv,
):
    nst, nz, wide = stage.shape[1], stage.shape[2], stage.shape[3]
    chunks = wide // rows
    me = lax.axis_index("interval")
    sl = lax.axis_index("slab")
    z_low = lax.rem(sl + slabs - 1, slabs)
    z_high = lax.rem(sl + 1, slabs)
    x_low = lax.rem(me + peers - 1, peers)
    x_high = lax.rem(me + 1, peers)
    order = [0] + ([chunks - 1] if chunks > 1 else []) + list(range(1, chunks - 1))

    def pull(k):
        start = pl.multiple_of(lax.rem(me + k, peers) * wide, 8)
        return pltpu.make_async_copy(
            states.at[:, :, pl.ds(start, wide), :], stage.at[k], in_sem.at[k]
        )

    for k in [*range(1, peers), 0]:
        pull(k).start()
    core_copy = pltpu.make_async_copy(
        core.at[:, pl.ds(pl.multiple_of(me * wide, 8), wide), :], core_v, core_sem
    )
    core_copy.start()

    barrier = pltpu.get_barrier_semaphore()
    for k in range(1, peers):
        pl.semaphore_signal(
            barrier, inc=1, device_id=(lax.rem(me + k, peers), sl), device_id_type=MESH
        )
    for z in (z_low, z_high):
        pl.semaphore_signal(barrier, inc=1, device_id=(me, z), device_id_type=MESH)

    weights = [occ[s].astype(jnp.float32) * (1.0 / denominator) for s in range(nst)]

    def term(k, at):
        total = None
        for s in range(nst):
            value = stage[k, s, :, pl.ds(at, edge), :]
            part = (weights[s] * value) * value
            total = part if total is None else total + part
        return total

    def tiles(c, body):
        def step(t, _):
            body(pl.multiple_of(c * rows + t * edge, edge))
            return 0

        lax.fori_loop(0, rows // edge, step, 0)

    def share(k, c):
        span = pl.ds(c * rows, rows)
        return pltpu.make_async_remote_copy(
            src_ref=snd.at[k - 1, :, span, :],
            dst_ref=rcv.at[k - 1, :, span, :],
            send_sem=rs_send.at[k - 1, c],
            recv_sem=rs_recv.at[k - 1, c],
            device_id=(lax.rem(me + k, peers), sl),
            device_id_type=MESH,
        )

    def planes(field, way, c):
        ref = (dens, fz)[field]
        pad = (edge, 0)[field]
        span = pl.ds(pad + c * rows, rows)
        source, target = ((2, nz + 2), (nz, 0))[way]
        return pltpu.make_async_remote_copy(
            src_ref=ref.at[pl.ds(source, 2), span, :],
            dst_ref=ref.at[pl.ds(target, 2), span, :],
            send_sem=z_send.at[field, way, c],
            recv_sem=z_recv.at[field, way, c],
            device_id=(me, (z_low, z_high)[way]),
            device_id_type=MESH,
        )

    def sides(field, way):
        ref = (dens.at[pl.ds(2, nz)], fx)[field]
        source, target = ((edge, edge + wide), (wide, 0))[way]
        return pltpu.make_async_remote_copy(
            src_ref=ref.at[:, pl.ds(source, edge), :],
            dst_ref=ref.at[:, pl.ds(target, edge), :],
            send_sem=x_send.at[field, way],
            recv_sem=x_recv.at[field, way],
            device_id=((x_low, x_high)[way], sl),
            device_id_type=MESH,
        )

    started = []

    def start(copy):
        copy.start()
        started.append(copy)

    first = True
    for c in order:
        for k in range(1, peers):
            if first:
                pull(k).wait()

            def fill(at, k=k):
                snd[k - 1, :, pl.ds(at, edge), :] = term(k, at)

            tiles(c, fill)
            if first and k == 1:
                pl.semaphore_wait(barrier, peers + 1)
            start(share(k, c))
        first = False
    pull(0).wait()
    core_copy.wait()

    def gather(c):
        for k in range(1, peers):
            share(k, c).wait_recv()

        def add(at):
            total = term(0, at)
            for k in range(1, peers):
                total = total + rcv[k - 1, :, pl.ds(at, edge), :]
            dens[2 : nz + 2, pl.ds(at + edge, edge), :] = (
                total + core_v[:, pl.ds(at, edge), :]
            )

        tiles(c, add)
        if c == 0:
            start(sides(0, 0))
        if c == chunks - 1:
            start(sides(0, 1))
        for way in (0, 1):
            start(planes(0, way, c))

    def energy(c):
        for way in (0, 1):
            planes(0, way, c).wait_recv()
        if c == chunks - 1:
            sides(0, 0).wait_recv()
        if c == 0:
            sides(0, 1).wait_recv()

        def work(at):
            inner = pl.ds(at + edge, edge)
            n = dens[2 : nz + 2, inner, :]
            grad_z = deriv_z(dens[:, inner, :])
            grad_x = deriv_x(dens[2 : nz + 2, pl.ds(at, 3 * edge), :])
            grad_y = deriv_y(n)
            g = grad_z * grad_z + grad_x * grad_x + grad_y * grad_y
            e_rho, e_grad = pbe_derivs(n, g)
            twice = 2.0 * e_grad
            fz[2 : nz + 2, pl.ds(at, edge), :] = twice * grad_z
            fx[:, inner, :] = twice * grad_x
            out[:, pl.ds(at, edge), :] = e_rho - deriv_y(twice * grad_y)

        tiles(c, work)
        if c == 0:
            start(sides(1, 0))
        if c == chunks - 1:
            start(sides(1, 1))
        for way in (0, 1):
            start(planes(1, way, c))

    def diverge(c):
        for way in (0, 1):
            planes(1, way, c).wait_recv()
        if c == chunks - 1:
            sides(1, 0).wait_recv()
        if c == 0:
            sides(1, 1).wait_recv()

        def work(at):
            span = pl.ds(at, edge)
            out[:, span, :] = out[:, span, :] - (
                deriv_z(fz[:, span, :]) + deriv_x(fx[:, pl.ds(at, 3 * edge), :])
            )

        tiles(c, work)

    gathered, done = set(), set()
    for c in order:
        gather(c)
        gathered.add(c)
        for d in order:
            near = {e for e in (d - 1, d, d + 1) if 0 <= e < chunks}
            ends = d not in (0, chunks - 1) or {0, chunks - 1} <= gathered
            if d not in done and near <= gathered and ends and len(gathered) > 2:
                energy(d)
                done.add(d)
                break
    for d in order:
        if d not in done:
            energy(d)
    for d in order:
        diverge(d)
    for copy in started:
        copy.wait_send()


def shards(peers, slabs, states, occupations, core_density):
    nst, nz, full, deep = states.shape
    wide = full // peers
    rows = 16 if wide % 16 == 0 else 8
    chunks = wide // rows
    f32 = jnp.float32
    dma = pltpu.SemaphoreType.DMA
    return pl.pallas_call(
        functools.partial(kernel, peers, slabs, rows),
        out_shape=jax.ShapeDtypeStruct((nz, wide, deep), f32),
        in_specs=[
            pl.BlockSpec(memory_space=pl.ANY),
            pl.BlockSpec(memory_space=pltpu.SMEM),
            pl.BlockSpec(memory_space=pl.ANY),
        ],
        out_specs=pl.BlockSpec(memory_space=pltpu.VMEM),
        scratch_shapes=[
            pltpu.VMEM((peers, nst, nz, wide, deep), f32),
            pltpu.VMEM((nz, wide, deep), f32),
            pltpu.VMEM((peers - 1, nz, wide, deep), f32),
            pltpu.VMEM((peers - 1, nz, wide, deep), f32),
            pltpu.VMEM((nz + 4, wide + 2 * edge, deep), f32),
            pltpu.VMEM((nz + 4, wide, deep), f32),
            pltpu.VMEM((nz, wide + 2 * edge, deep), f32),
            dma((peers,)),
            dma,
            dma((peers - 1, chunks)),
            dma((peers - 1, chunks)),
            dma((2, 2, chunks)),
            dma((2, 2, chunks)),
            dma((2, 2)),
            dma((2, 2)),
        ],
        compiler_params=pltpu.CompilerParams(
            collective_id=0, has_side_effects=True, vmem_limit_bytes=67043328 - 640 * 1024
        ),
    )(states, occupations, core_density)


def solution(mesh):
    return jax.shard_map(
        functools.partial(shards, mesh.shape["interval"], mesh.shape["slab"]),
        mesh=mesh,
        in_specs=(P("interval", "slab", None, None), P("interval"), P("slab", None, None)),
        out_specs=P("slab", "interval", None),
        check_vma=False,
    )
```

```python
import functools
import math

import jax
import jax.numpy as jnp
from jax import lax
from jax.experimental import pallas as pl
from jax.experimental.pallas import tpu as pltpu
from jax.sharding import PartitionSpec as P

spacing = 0.25
denominator = 64.0
pbe_kappa = 0.804
pbe_mu = 0.2195149727645171
pbe_beta = 0.06672455060314922
pw_alpha = 0.0310907
pbe_gamma = (1.0 - math.log(2.0)) / math.pi**2
MESH = pl.DeviceIdType.MESH
edge = 8


def five_point(low2, low1, high1, high2):
    return (8.0 * (high1 - low1) - (high2 - low2)) * (1.0 / (12.0 * spacing))


def deriv_y(field):
    axis = field.ndim - 1
    count = field.shape[axis]
    return five_point(
        pltpu.roll(field, 2, axis),
        pltpu.roll(field, 1, axis),
        pltpu.roll(field, count - 1, axis),
        pltpu.roll(field, count - 2, axis),
    )


def deriv_x(tall):
    return five_point(
        tall[:, edge - 2 : -edge - 2],
        tall[:, edge - 1 : -edge - 1],
        tall[:, edge + 1 : 1 - edge],
        tall[:, edge + 2 : 2 - edge],
    )


def deriv_z(tall):
    count = tall.shape[0] - 4
    return five_point(
        tall[:count], tall[1 : count + 1], tall[3 : count + 3], tall[4 : count + 4]
    )


def pbe_derivs(n, g):
    k_one = (3.0 * math.pi**2) ** (1.0 / 3.0)
    ex_one = -0.75 * (3.0 / math.pi) ** (1.0 / 3.0)
    r_one = (3.0 / (4.0 * math.pi)) ** (1.0 / 3.0)
    s_one = 1.0 / (4.0 * k_one**2)
    t_one = math.pi / (16.0 * k_one)
    ratio = pbe_beta / pbe_gamma
    inv_six = jnp.exp(jnp.log(n) * (-1.0 / 6.0))
    inv = inv_six * inv_six
    inv2 = inv * inv
    inv4 = inv2 * inv2
    cube = n * inv2
    s_sq = (s_one * g) * (inv4 * inv4)
    u_inv = 1.0 / (1.0 + (pbe_mu / pbe_kappa) * s_sq)
    f_exch = (1.0 + pbe_kappa) - pbe_kappa * u_inv
    f_slope = pbe_mu * u_inv * u_inv
    ex_rho = (ex_one * cube) * ((4.0 / 3.0) * f_exch - (8.0 / 3.0) * f_slope * s_sq)

    radius = r_one * inv
    root = math.sqrt(r_one) * inv_six
    two_a = 2.0 * pw_alpha
    lower = (two_a * root) * (
        7.5957 + root * (3.5876 + root * (1.6382 + root * 0.49294))
    )
    slope = (two_a * root) * (
        0.5 * 7.5957 + root * (3.5876 + root * (1.5 * 1.6382 + root * (2.0 * 0.49294)))
    )
    pair_inv = 1.0 / (lower * (lower + 1.0))
    log_term = jnp.log(1.0 + (lower + 1.0) * pair_inv)
    front = two_a + (two_a * 0.2137) * radius
    e_corr = -front * log_term
    n_ec = (1.0 / 3.0) * ((two_a * 0.2137) * radius * log_term - front * slope * pair_inv)

    grown = jnp.exp(e_corr * (-1.0 / pbe_gamma))
    factor = ratio / (grown - 1.0)
    t_sq = (t_one * g) * (inv4 * inv2 * inv)
    y = factor * t_sq
    lift = 1.0 + y
    den = lift + y * y
    add = (ratio * t_sq) * lift
    full = den + add
    inv_full = 1.0 / (den * full)
    h_term = pbe_gamma * jnp.log(1.0 + add * (full * inv_full))
    h_t = (pbe_beta * inv_full) * (1.0 + 2.0 * y)
    h_ec = -(y * y) * (y * (2.0 + y)) * inv_full * grown
    e_rho = ex_rho + e_corr + h_term + n_ec + h_ec * n_ec - (7.0 / 3.0) * (t_sq * h_t)
    e_grad = inv4 * (t_one * h_t + (ex_one * s_one) * f_slope)
    return e_rho, e_grad


def kernel(
    peers, slabs, rows,
    states, occ, core, out,
    stage, core_v, snd, rcv, dens, fz, fx,
    in_sem, core_sem, rs_send, rs_recv, z_send, z_recv, x_send, x_recv,
):
    nst, nz, wide = stage.shape[1], stage.shape[2], stage.shape[3]
    chunks = wide // rows
    me = lax.axis_index("interval")
    sl = lax.axis_index("slab")
    z_low = lax.rem(sl + slabs - 1, slabs)
    z_high = lax.rem(sl + 1, slabs)
    x_low = lax.rem(me + peers - 1, peers)
    x_high = lax.rem(me + 1, peers)
    order = [0] + ([chunks - 1] if chunks > 1 else []) + list(range(1, chunks - 1))

    def pull(k):
        start = pl.multiple_of(lax.rem(me + k, peers) * wide, 8)
        return pltpu.make_async_copy(
            states.at[:, :, pl.ds(start, wide), :], stage.at[k], in_sem.at[k]
        )

    for k in [*range(1, peers), 0]:
        pull(k).start()
    core_copy = pltpu.make_async_copy(
        core.at[:, pl.ds(pl.multiple_of(me * wide, 8), wide), :], core_v, core_sem
    )
    core_copy.start()

    barrier = pltpu.get_barrier_semaphore()
    for k in range(1, peers):
        pl.semaphore_signal(
            barrier, inc=1, device_id=(lax.rem(me + k, peers), sl), device_id_type=MESH
        )
    for z in (z_low, z_high):
        pl.semaphore_signal(barrier, inc=1, device_id=(me, z), device_id_type=MESH)

    weights = [occ[s].astype(jnp.float32) * (1.0 / denominator) for s in range(nst)]

    def term(k, at):
        total = None
        for s in range(nst):
            value = stage[k, s, :, pl.ds(at, edge), :]
            part = (weights[s] * value) * value
            total = part if total is None else total + part
        return total

    def tiles(c, body):
        def step(t, _):
            body(pl.multiple_of(c * rows + t * edge, edge))
            return 0

        lax.fori_loop(0, rows // edge, step, 0)

    def share(k, c):
        span = pl.ds(c * rows, rows)
        return pltpu.make_async_remote_copy(
            src_ref=snd.at[k - 1, :, span, :],
            dst_ref=rcv.at[k - 1, :, span, :],
            send_sem=rs_send.at[k - 1, c],
            recv_sem=rs_recv.at[k - 1, c],
            device_id=(lax.rem(me + k, peers), sl),
            device_id_type=MESH,
        )

    def planes(field, way, c):
        ref = (dens, fz)[field]
        pad = (edge, 0)[field]
        span = pl.ds(pad + c * rows, rows)
        source, target = ((2, nz + 2), (nz, 0))[way]
        return pltpu.make_async_remote_copy(
            src_ref=ref.at[pl.ds(source, 2), span, :],
            dst_ref=ref.at[pl.ds(target, 2), span, :],
            send_sem=z_send.at[field, way, c],
            recv_sem=z_recv.at[field, way, c],
            device_id=(me, (z_low, z_high)[way]),
            device_id_type=MESH,
        )

    def sides(field, way):
        ref = (dens.at[pl.ds(2, nz)], fx)[field]
        source, target = ((edge, edge + wide), (wide, 0))[way]
        return pltpu.make_async_remote_copy(
            src_ref=ref.at[:, pl.ds(source, edge), :],
            dst_ref=ref.at[:, pl.ds(target, edge), :],
            send_sem=x_send.at[field, way],
            recv_sem=x_recv.at[field, way],
            device_id=((x_low, x_high)[way], sl),
            device_id_type=MESH,
        )

    started = []

    def start(copy):
        copy.start()
        started.append(copy)

    first = True
    for c in order:
        for k in range(1, peers):
            if first:
                pull(k).wait()

            def fill(at, k=k):
                snd[k - 1, :, pl.ds(at, edge), :] = term(k, at)

            tiles(c, fill)
            if first and k == 1:
                pl.semaphore_wait(barrier, peers + 1)
            start(share(k, c))
        first = False
    pull(0).wait()
    core_copy.wait()

    def gather(c):
        for k in range(1, peers):
            share(k, c).wait_recv()

        def add(at):
            total = term(0, at)
            for k in range(1, peers):
                total = total + rcv[k - 1, :, pl.ds(at, edge), :]
            dens[2 : nz + 2, pl.ds(at + edge, edge), :] = (
                total + core_v[:, pl.ds(at, edge), :]
            )

        tiles(c, add)
        if c == 0:
            start(sides(0, 0))
        if c == chunks - 1:
            start(sides(0, 1))
        for way in (0, 1):
            start(planes(0, way, c))

    def energy(c):
        for way in (0, 1):
            planes(0, way, c).wait_recv()
        if c == chunks - 1:
            sides(0, 0).wait_recv()
        if c == 0:
            sides(0, 1).wait_recv()

        def work(at):
            inner = pl.ds(at + edge, edge)
            n = dens[2 : nz + 2, inner, :]
            grad_z = deriv_z(dens[:, inner, :])
            grad_x = deriv_x(dens[2 : nz + 2, pl.ds(at, 3 * edge), :])
            grad_y = deriv_y(n)
            g = grad_z * grad_z + grad_x * grad_x + grad_y * grad_y
            e_rho, e_grad = pbe_derivs(n, g)
            twice = 2.0 * e_grad
            fz[2 : nz + 2, pl.ds(at, edge), :] = twice * grad_z
            fx[:, inner, :] = twice * grad_x
            out[:, pl.ds(at, edge), :] = e_rho - deriv_y(twice * grad_y)

        tiles(c, work)
        if c == 0:
            start(sides(1, 0))
        if c == chunks - 1:
            start(sides(1, 1))
        for way in (0, 1):
            start(planes(1, way, c))

    def diverge(c):
        for way in (0, 1):
            planes(1, way, c).wait_recv()
        if c == chunks - 1:
            sides(1, 0).wait_recv()
        if c == 0:
            sides(1, 1).wait_recv()

        def work(at):
            span = pl.ds(at, edge)
            out[:, span, :] = out[:, span, :] - (
                deriv_z(fz[:, span, :]) + deriv_x(fx[:, pl.ds(at, 3 * edge), :])
            )

        tiles(c, work)

    gathered, done = set(), set()
    for c in order:
        gather(c)
        gathered.add(c)
        for d in order:
            near = {e for e in (d - 1, d, d + 1) if 0 <= e < chunks}
            ends = d not in (0, chunks - 1) or {0, chunks - 1} <= gathered
            if d not in done and near <= gathered and ends and len(gathered) > 2:
                energy(d)
                done.add(d)
                break
    for d in order:
        if d not in done:
            energy(d)
    for d in order:
        diverge(d)
    for copy in started:
        copy.wait_send()


def shards(peers, slabs, states, occupations, core_density):
    nst, nz, full, deep = states.shape
    wide = full // peers
    rows = 32 if wide % 32 == 0 else 8
    chunks = wide // rows
    f32 = jnp.float32
    dma = pltpu.SemaphoreType.DMA
    return pl.pallas_call(
        functools.partial(kernel, peers, slabs, rows),
        out_shape=jax.ShapeDtypeStruct((nz, wide, deep), f32),
        in_specs=[
            pl.BlockSpec(memory_space=pl.ANY),
            pl.BlockSpec(memory_space=pltpu.SMEM),
            pl.BlockSpec(memory_space=pl.ANY),
        ],
        out_specs=pl.BlockSpec(memory_space=pltpu.VMEM),
        scratch_shapes=[
            pltpu.VMEM((peers, nst, nz, wide, deep), f32),
            pltpu.VMEM((nz, wide, deep), f32),
            pltpu.VMEM((peers - 1, nz, wide, deep), f32),
            pltpu.VMEM((peers - 1, nz, wide, deep), f32),
            pltpu.VMEM((nz + 4, wide + 2 * edge, deep), f32),
            pltpu.VMEM((nz + 4, wide, deep), f32),
            pltpu.VMEM((nz, wide + 2 * edge, deep), f32),
            dma((peers,)),
            dma,
            dma((peers - 1, chunks)),
            dma((peers - 1, chunks)),
            dma((2, 2, chunks)),
            dma((2, 2, chunks)),
            dma((2, 2)),
            dma((2, 2)),
        ],
        compiler_params=pltpu.CompilerParams(
            collective_id=0, has_side_effects=True, vmem_limit_bytes=67043328 - 1000 * 1024
        ),
    )(states, occupations, core_density)


def solution(mesh):
    return jax.shard_map(
        functools.partial(shards, mesh.shape["interval"], mesh.shape["slab"]),
        mesh=mesh,
        in_specs=(P("interval", "slab", None, None), P("interval"), P("slab", None, None)),
        out_specs=P("slab", "interval", None),
        check_vma=False,
    )
```

```python
import functools
import math

import jax
import jax.numpy as jnp
from jax import lax
from jax.experimental import pallas as pl
from jax.experimental.pallas import tpu as pltpu
from jax.sharding import PartitionSpec as P

spacing = 0.25
denominator = 64.0
pbe_kappa = 0.804
pbe_mu = 0.2195149727645171
pbe_beta = 0.06672455060314922
pw_alpha = 0.0310907
pbe_gamma = (1.0 - math.log(2.0)) / math.pi**2
MESH = pl.DeviceIdType.MESH
edge = 8


def five_point(low2, low1, high1, high2):
    return (8.0 * (high1 - low1) - (high2 - low2)) * (1.0 / (12.0 * spacing))


def deriv_y(field):
    axis = field.ndim - 1
    count = field.shape[axis]
    return five_point(
        pltpu.roll(field, 2, axis),
        pltpu.roll(field, 1, axis),
        pltpu.roll(field, count - 1, axis),
        pltpu.roll(field, count - 2, axis),
    )


def deriv_x(tall):
    return five_point(
        tall[:, edge - 2 : -edge - 2],
        tall[:, edge - 1 : -edge - 1],
        tall[:, edge + 1 : 1 - edge],
        tall[:, edge + 2 : 2 - edge],
    )


def deriv_z(tall):
    count = tall.shape[0] - 4
    return five_point(
        tall[:count], tall[1 : count + 1], tall[3 : count + 3], tall[4 : count + 4]
    )


def pbe_derivs(n, g):
    k_one = (3.0 * math.pi**2) ** (1.0 / 3.0)
    ex_one = -0.75 * (3.0 / math.pi) ** (1.0 / 3.0)
    r_one = (3.0 / (4.0 * math.pi)) ** (1.0 / 3.0)
    s_one = 1.0 / (4.0 * k_one**2)
    t_one = math.pi / (16.0 * k_one)
    ratio = pbe_beta / pbe_gamma
    inv_six = jnp.exp(jnp.log(n) * (-1.0 / 6.0))
    inv = inv_six * inv_six
    inv2 = inv * inv
    inv4 = inv2 * inv2
    cube = n * inv2
    s_sq = (s_one * g) * (inv4 * inv4)
    u_inv = 1.0 / (1.0 + (pbe_mu / pbe_kappa) * s_sq)
    f_exch = (1.0 + pbe_kappa) - pbe_kappa * u_inv
    f_slope = pbe_mu * u_inv * u_inv
    ex_rho = (ex_one * cube) * ((4.0 / 3.0) * f_exch - (8.0 / 3.0) * f_slope * s_sq)

    radius = r_one * inv
    root = math.sqrt(r_one) * inv_six
    two_a = 2.0 * pw_alpha
    lower = (two_a * root) * (
        7.5957 + root * (3.5876 + root * (1.6382 + root * 0.49294))
    )
    slope = (two_a * root) * (
        0.5 * 7.5957 + root * (3.5876 + root * (1.5 * 1.6382 + root * (2.0 * 0.49294)))
    )
    pair_inv = 1.0 / (lower * (lower + 1.0))
    log_term = jnp.log(1.0 + (lower + 1.0) * pair_inv)
    front = two_a + (two_a * 0.2137) * radius
    e_corr = -front * log_term
    n_ec = (1.0 / 3.0) * ((two_a * 0.2137) * radius * log_term - front * slope * pair_inv)

    grown = jnp.exp(e_corr * (-1.0 / pbe_gamma))
    factor = ratio / (grown - 1.0)
    t_sq = (t_one * g) * (inv4 * inv2 * inv)
    y = factor * t_sq
    lift = 1.0 + y
    den = lift + y * y
    add = (ratio * t_sq) * lift
    full = den + add
    inv_full = 1.0 / (den * full)
    h_term = pbe_gamma * jnp.log(1.0 + add * (full * inv_full))
    h_t = (pbe_beta * inv_full) * (1.0 + 2.0 * y)
    h_ec = -(y * y) * (y * (2.0 + y)) * inv_full * grown
    e_rho = ex_rho + e_corr + h_term + n_ec + h_ec * n_ec - (7.0 / 3.0) * (t_sq * h_t)
    e_grad = inv4 * (t_one * h_t + (ex_one * s_one) * f_slope)
    return e_rho, e_grad


def kernel(
    peers, slabs, rows,
    states, occ, core, out,
    stage, core_v, snd, rcv, dens, fz, fx,
    in_sem, core_sem, rs_send, rs_recv, z_send, z_recv, x_send, x_recv,
):
    nst, nz, wide = stage.shape[1], stage.shape[2], stage.shape[3]
    chunks = wide // rows
    me = lax.axis_index("interval")
    sl = lax.axis_index("slab")
    z_low = lax.rem(sl + slabs - 1, slabs)
    z_high = lax.rem(sl + 1, slabs)
    x_low = lax.rem(me + peers - 1, peers)
    x_high = lax.rem(me + 1, peers)
    order = [0] + ([chunks - 1] if chunks > 1 else []) + list(range(1, chunks - 1))

    def pull(k):
        start = pl.multiple_of(lax.rem(me + k, peers) * wide, 8)
        return pltpu.make_async_copy(
            states.at[:, :, pl.ds(start, wide), :], stage.at[k], in_sem.at[k]
        )

    for k in [*range(1, peers), 0]:
        pull(k).start()
    core_copy = pltpu.make_async_copy(
        core.at[:, pl.ds(pl.multiple_of(me * wide, 8), wide), :], core_v, core_sem
    )
    core_copy.start()

    barrier = pltpu.get_barrier_semaphore()
    for k in range(1, peers):
        pl.semaphore_signal(
            barrier, inc=1, device_id=(lax.rem(me + k, peers), sl), device_id_type=MESH
        )
    for z in (z_low, z_high):
        pl.semaphore_signal(barrier, inc=1, device_id=(me, z), device_id_type=MESH)

    weights = [occ[s].astype(jnp.float32) * (1.0 / denominator) for s in range(nst)]

    def term(k, at):
        total = None
        for s in range(nst):
            value = stage[k, s, :, pl.ds(at, edge), :]
            part = (weights[s] * value) * value
            total = part if total is None else total + part
        return total

    def tiles(c, body):
        def step(t, _):
            body(pl.multiple_of(c * rows + t * edge, edge))
            return 0

        lax.fori_loop(0, rows // edge, step, 0)

    def share(k, c):
        span = pl.ds(c * rows, rows)
        return pltpu.make_async_remote_copy(
            src_ref=snd.at[k - 1, :, span, :],
            dst_ref=rcv.at[k - 1, :, span, :],
            send_sem=rs_send.at[k - 1, c],
            recv_sem=rs_recv.at[k - 1, c],
            device_id=(lax.rem(me + k, peers), sl),
            device_id_type=MESH,
        )

    def planes(field, way, c):
        ref = (dens, fz)[field]
        pad = (edge, 0)[field]
        span = pl.ds(pad + c * rows, rows)
        source, target = ((2, nz + 2), (nz, 0))[way]
        return pltpu.make_async_remote_copy(
            src_ref=ref.at[pl.ds(source, 2), span, :],
            dst_ref=ref.at[pl.ds(target, 2), span, :],
            send_sem=z_send.at[field, way, c],
            recv_sem=z_recv.at[field, way, c],
            device_id=(me, (z_low, z_high)[way]),
            device_id_type=MESH,
        )

    def sides(field, way):
        ref = (dens.at[pl.ds(2, nz)], fx)[field]
        source, target = ((edge, edge + wide), (wide, 0))[way]
        return pltpu.make_async_remote_copy(
            src_ref=ref.at[:, pl.ds(source, edge), :],
            dst_ref=ref.at[:, pl.ds(target, edge), :],
            send_sem=x_send.at[field, way],
            recv_sem=x_recv.at[field, way],
            device_id=((x_low, x_high)[way], sl),
            device_id_type=MESH,
        )

    started = []

    def start(copy):
        copy.start()
        started.append(copy)

    first = True
    for c in order:
        for k in range(1, peers):
            if first:
                pull(k).wait()

            def fill(at, k=k):
                snd[k - 1, :, pl.ds(at, edge), :] = term(k, at)

            tiles(c, fill)
            if first and k == 1:
                pl.semaphore_wait(barrier, peers + 1)
            start(share(k, c))
        first = False
    pull(0).wait()
    core_copy.wait()

    def gather(c):
        for k in range(1, peers):
            share(k, c).wait_recv()

        def add(at):
            total = term(0, at)
            for k in range(1, peers):
                total = total + rcv[k - 1, :, pl.ds(at, edge), :]
            dens[2 : nz + 2, pl.ds(at + edge, edge), :] = (
                total + core_v[:, pl.ds(at, edge), :]
            )

        tiles(c, add)
        if c == 0:
            start(sides(0, 0))
        if c == chunks - 1:
            start(sides(0, 1))
        for way in (0, 1):
            start(planes(0, way, c))

    def energy(c):
        for way in (0, 1):
            planes(0, way, c).wait_recv()
        if c == chunks - 1:
            sides(0, 0).wait_recv()
        if c == 0:
            sides(0, 1).wait_recv()

        def work(at):
            inner = pl.ds(at + edge, edge)
            n = dens[2 : nz + 2, inner, :]
            grad_z = deriv_z(dens[:, inner, :])
            grad_x = deriv_x(dens[2 : nz + 2, pl.ds(at, 3 * edge), :])
            grad_y = deriv_y(n)
            g = grad_z * grad_z + grad_x * grad_x + grad_y * grad_y
            e_rho, e_grad = pbe_derivs(n, g)
            twice = 2.0 * e_grad
            fz[2 : nz + 2, pl.ds(at, edge), :] = twice * grad_z
            fx[:, inner, :] = twice * grad_x
            out[:, pl.ds(at, edge), :] = e_rho - deriv_y(twice * grad_y)

        tiles(c, work)
        if c == 0:
            start(sides(1, 0))
        if c == chunks - 1:
            start(sides(1, 1))
        for way in (0, 1):
            start(planes(1, way, c))

    def diverge(c):
        for way in (0, 1):
            planes(1, way, c).wait_recv()
        if c == chunks - 1:
            sides(1, 0).wait_recv()
        if c == 0:
            sides(1, 1).wait_recv()

        def work(at):
            span = pl.ds(at, edge)
            out[:, span, :] = out[:, span, :] - (
                deriv_z(fz[:, span, :]) + deriv_x(fx[:, pl.ds(at, 3 * edge), :])
            )

        tiles(c, work)

    gathered, done = set(), set()
    for c in order:
        gather(c)
        gathered.add(c)
        for d in order:
            near = {e for e in (d - 1, d, d + 1) if 0 <= e < chunks}
            ends = d not in (0, chunks - 1) or {0, chunks - 1} <= gathered
            if d not in done and near <= gathered and ends and len(gathered) > 2:
                energy(d)
                done.add(d)
                break
    for d in order:
        if d not in done:
            energy(d)
    for d in order:
        diverge(d)
    for copy in started:
        copy.wait_send()


def shards(peers, slabs, states, occupations, core_density):
    nst, nz, full, deep = states.shape
    wide = full // peers
    rows = 16 if wide % 16 == 0 else 8
    chunks = wide // rows
    f32 = jnp.float32
    dma = pltpu.SemaphoreType.DMA
    return pl.pallas_call(
        functools.partial(kernel, peers, slabs, rows),
        out_shape=jax.ShapeDtypeStruct((nz, wide, deep), f32),
        in_specs=[
            pl.BlockSpec(memory_space=pltpu.HBM),
            pl.BlockSpec(memory_space=pltpu.SMEM),
            pl.BlockSpec(memory_space=pltpu.HBM),
        ],
        out_specs=pl.BlockSpec(memory_space=pltpu.VMEM),
        scratch_shapes=[
            pltpu.VMEM((peers, nst, nz, wide, deep), f32),
            pltpu.VMEM((nz, wide, deep), f32),
            pltpu.VMEM((peers - 1, nz, wide, deep), f32),
            pltpu.VMEM((peers - 1, nz, wide, deep), f32),
            pltpu.VMEM((nz + 4, wide + 2 * edge, deep), f32),
            pltpu.VMEM((nz + 4, wide, deep), f32),
            pltpu.VMEM((nz, wide + 2 * edge, deep), f32),
            dma((peers,)),
            dma,
            dma((peers - 1, chunks)),
            dma((peers - 1, chunks)),
            dma((2, 2, chunks)),
            dma((2, 2, chunks)),
            dma((2, 2)),
            dma((2, 2)),
        ],
        compiler_params=pltpu.CompilerParams(
            collective_id=0, has_side_effects=True, vmem_limit_bytes=48 * 1024 * 1024
        ),
    )(states, occupations, core_density)


def solution(mesh):
    return jax.shard_map(
        functools.partial(shards, mesh.shape["interval"], mesh.shape["slab"]),
        mesh=mesh,
        in_specs=(P("interval", "slab", None, None), P("interval"), P("slab", None, None)),
        out_specs=P("slab", "interval", None),
        check_vma=False,
    )
```

```python
import functools
import math

import jax
import jax.numpy as jnp
from jax import lax
from jax.experimental import pallas as pl
from jax.experimental.pallas import tpu as pltpu
from jax.sharding import PartitionSpec as P

spacing = 0.25
denominator = 64.0
pbe_kappa = 0.804
pbe_mu = 0.2195149727645171
pbe_beta = 0.06672455060314922
pw_alpha = 0.0310907
pbe_gamma = (1.0 - math.log(2.0)) / math.pi**2
MESH = pl.DeviceIdType.MESH
edge = 8


def five_point(low2, low1, high1, high2):
    return (8.0 * (high1 - low1) - (high2 - low2)) * (1.0 / (12.0 * spacing))


def deriv_y(field):
    axis = field.ndim - 1
    count = field.shape[axis]
    return five_point(
        pltpu.roll(field, 2, axis),
        pltpu.roll(field, 1, axis),
        pltpu.roll(field, count - 1, axis),
        pltpu.roll(field, count - 2, axis),
    )


def deriv_x(tall):
    return five_point(
        tall[:, edge - 2 : -edge - 2],
        tall[:, edge - 1 : -edge - 1],
        tall[:, edge + 1 : 1 - edge],
        tall[:, edge + 2 : 2 - edge],
    )


def deriv_z(tall):
    count = tall.shape[0] - 4
    return five_point(
        tall[:count], tall[1 : count + 1], tall[3 : count + 3], tall[4 : count + 4]
    )


def pbe_derivs(n, g):
    k_one = (3.0 * math.pi**2) ** (1.0 / 3.0)
    ex_one = -0.75 * (3.0 / math.pi) ** (1.0 / 3.0)
    r_one = (3.0 / (4.0 * math.pi)) ** (1.0 / 3.0)
    s_one = 1.0 / (4.0 * k_one**2)
    t_one = math.pi / (16.0 * k_one)
    ratio = pbe_beta / pbe_gamma
    inv_six = jnp.exp(jnp.log(n) * (-1.0 / 6.0))
    inv = inv_six * inv_six
    inv2 = inv * inv
    inv4 = inv2 * inv2
    cube = n * inv2
    s_sq = (s_one * g) * (inv4 * inv4)
    u_inv = 1.0 / (1.0 + (pbe_mu / pbe_kappa) * s_sq)
    f_exch = (1.0 + pbe_kappa) - pbe_kappa * u_inv
    f_slope = pbe_mu * u_inv * u_inv
    ex_rho = (ex_one * cube) * ((4.0 / 3.0) * f_exch - (8.0 / 3.0) * f_slope * s_sq)

    radius = r_one * inv
    root = math.sqrt(r_one) * inv_six
    two_a = 2.0 * pw_alpha
    lower = (two_a * root) * (
        7.5957 + root * (3.5876 + root * (1.6382 + root * 0.49294))
    )
    slope = (two_a * root) * (
        0.5 * 7.5957 + root * (3.5876 + root * (1.5 * 1.6382 + root * (2.0 * 0.49294)))
    )
    pair_inv = 1.0 / (lower * (lower + 1.0))
    log_term = jnp.log(1.0 + (lower + 1.0) * pair_inv)
    front = two_a + (two_a * 0.2137) * radius
    e_corr = -front * log_term
    n_ec = (1.0 / 3.0) * ((two_a * 0.2137) * radius * log_term - front * slope * pair_inv)

    grown = jnp.exp(e_corr * (-1.0 / pbe_gamma))
    factor = ratio / (grown - 1.0)
    t_sq = (t_one * g) * (inv4 * inv2 * inv)
    y = factor * t_sq
    lift = 1.0 + y
    den = lift + y * y
    add = (ratio * t_sq) * lift
    full = den + add
    inv_full = 1.0 / (den * full)
    h_term = pbe_gamma * jnp.log(1.0 + add * (full * inv_full))
    h_t = (pbe_beta * inv_full) * (1.0 + 2.0 * y)
    h_ec = -(y * y) * (y * (2.0 + y)) * inv_full * grown
    e_rho = ex_rho + e_corr + h_term + n_ec + h_ec * n_ec - (7.0 / 3.0) * (t_sq * h_t)
    e_grad = inv4 * (t_one * h_t + (ex_one * s_one) * f_slope)
    return e_rho, e_grad


def kernel(
    peers, slabs, rows,
    states, occ, core, out,
    stage, core_v, snd, rcv, pair_out, pair_in, dens, fz, fx,
    in_sem, core_sem, rs_send, rs_recv, pair_send, pair_recv, z_send, z_recv, x_send, x_recv,
):
    nst, nz, wide = stage.shape[1], stage.shape[2], stage.shape[3]
    chunks = wide // rows
    me = lax.axis_index("interval")
    sl = lax.axis_index("slab")
    z_low = lax.rem(sl + slabs - 1, slabs)
    z_high = lax.rem(sl + 1, slabs)
    x_low = lax.rem(me + peers - 1, peers)
    x_high = lax.rem(me + 1, peers)
    square = peers == 4
    if square:
        hi, lo = lax.div(me, 2), lax.rem(me, 2)
        peer = [me, me + 1 - 2 * lo, me + 2 - 4 * hi, 3 - me]
    else:
        peer = [lax.rem(me + k, peers) for k in range(peers)]
    order = [0] + ([chunks - 1] if chunks > 1 else []) + list(range(1, chunks - 1))

    def pull(k):
        start = pl.multiple_of(peer[k] * wide, 8)
        return pltpu.make_async_copy(
            states.at[:, :, pl.ds(start, wide), :], stage.at[k], in_sem.at[k]
        )

    for k in [*range(1, peers), 0]:
        pull(k).start()
    core_copy = pltpu.make_async_copy(
        core.at[:, pl.ds(pl.multiple_of(me * wide, 8), wide), :], core_v, core_sem
    )
    core_copy.start()

    barrier = pltpu.get_barrier_semaphore()
    for k in range(1, peers):
        pl.semaphore_signal(
            barrier, inc=1, device_id=(peer[k], sl), device_id_type=MESH
        )
    for z in (z_low, z_high):
        pl.semaphore_signal(barrier, inc=1, device_id=(me, z), device_id_type=MESH)

    weights = [occ[s].astype(jnp.float32) * (1.0 / denominator) for s in range(nst)]

    def term(k, at):
        total = None
        for s in range(nst):
            value = stage[k, s, :, pl.ds(at, edge), :]
            part = (weights[s] * value) * value
            total = part if total is None else total + part
        return total

    def tiles(c, body):
        def step(t, _):
            body(pl.multiple_of(c * rows + t * edge, edge))
            return 0

        lax.fori_loop(0, rows // edge, step, 0)

    def share(k, c):
        span = pl.ds(c * rows, rows)
        return pltpu.make_async_remote_copy(
            src_ref=snd.at[k - 1, :, span, :],
            dst_ref=rcv.at[k - 1, :, span, :],
            send_sem=rs_send.at[k - 1, c],
            recv_sem=rs_recv.at[k - 1, c],
            device_id=(peer[k], sl),
            device_id_type=MESH,
        )

    def planes(field, way, c):
        ref = (dens, fz)[field]
        pad = (edge, 0)[field]
        span = pl.ds(pad + c * rows, rows)
        source, target = ((2, nz + 2), (nz, 0))[way]
        return pltpu.make_async_remote_copy(
            src_ref=ref.at[pl.ds(source, 2), span, :],
            dst_ref=ref.at[pl.ds(target, 2), span, :],
            send_sem=z_send.at[field, way, c],
            recv_sem=z_recv.at[field, way, c],
            device_id=(me, (z_low, z_high)[way]),
            device_id_type=MESH,
        )

    def sides(field, way):
        ref = (dens.at[pl.ds(2, nz)], fx)[field]
        source, target = ((edge, edge + wide), (wide, 0))[way]
        return pltpu.make_async_remote_copy(
            src_ref=ref.at[:, pl.ds(source, edge), :],
            dst_ref=ref.at[:, pl.ds(target, edge), :],
            send_sem=x_send.at[field, way],
            recv_sem=x_recv.at[field, way],
            device_id=((x_low, x_high)[way], sl),
            device_id_type=MESH,
        )

    started = []

    def start(copy):
        copy.start()
        started.append(copy)

    def near(c):
        return 1 + order.index(c) % 2

    def both(c):
        return pltpu.make_async_remote_copy(
            src_ref=pair_out.at[c],
            dst_ref=pair_in.at[c],
            send_sem=pair_send.at[c],
            recv_sem=pair_recv.at[c],
            device_id=(peer[near(c)], sl),
            device_id_type=MESH,
        )

    def relay(c):
        both(c).wait_recv()
        k = 3 - near(c)

        def fill(at):
            passed = pair_in[c, 1, :, pl.ds(pl.multiple_of(at - c * rows, edge), edge), :]
            snd[k - 1, :, pl.ds(at, edge), :] = term(k, at) + passed

        tiles(c, fill)
        start(share(k, c))

    if square:
        for k in range(1, peers):
            pull(k).wait()
        for c in order:

            def fill(at, c=c):
                here = pl.ds(pl.multiple_of(at - c * rows, edge), edge)
                pair_out[c, 0, :, here, :] = term(near(c), at)
                pair_out[c, 1, :, here, :] = term(3, at)

            tiles(c, fill)
            if c == order[0]:
                pl.semaphore_wait(barrier, peers + 1)
            start(both(c))
    first = not square
    for c in [] if square else order:
        for k in range(1, peers):
            if first:
                pull(k).wait()

            def fill(at, k=k):
                snd[k - 1, :, pl.ds(at, edge), :] = term(k, at)

            tiles(c, fill)
            if first and k == 1:
                pl.semaphore_wait(barrier, peers + 1)
            start(share(k, c))
        first = False
    pull(0).wait()
    core_copy.wait()

    def gather(c):
        arrived = [3 - near(c)] if square else list(range(1, peers))
        for k in arrived:
            share(k, c).wait_recv()

        def add(at):
            total = term(0, at)
            if square:
                total = total + pair_in[c, 0, :, pl.ds(pl.multiple_of(at - c * rows, edge), edge), :]
            for k in arrived:
                total = total + rcv[k - 1, :, pl.ds(at, edge), :]
            dens[2 : nz + 2, pl.ds(at + edge, edge), :] = (
                total + core_v[:, pl.ds(at, edge), :]
            )

        tiles(c, add)
        if c == 0:
            start(sides(0, 0))
        if c == chunks - 1:
            start(sides(0, 1))
        for way in (0, 1):
            start(planes(0, way, c))

    def energy(c):
        for way in (0, 1):
            planes(0, way, c).wait_recv()
        if c == chunks - 1:
            sides(0, 0).wait_recv()
        if c == 0:
            sides(0, 1).wait_recv()

        def work(at):
            inner = pl.ds(at + edge, edge)
            n = dens[2 : nz + 2, inner, :]
            grad_z = deriv_z(dens[:, inner, :])
            grad_x = deriv_x(dens[2 : nz + 2, pl.ds(at, 3 * edge), :])
            grad_y = deriv_y(n)
            g = grad_z * grad_z + grad_x * grad_x + grad_y * grad_y
            e_rho, e_grad = pbe_derivs(n, g)
            twice = 2.0 * e_grad
            fz[2 : nz + 2, pl.ds(at, edge), :] = twice * grad_z
            fx[:, inner, :] = twice * grad_x
            out[:, pl.ds(at, edge), :] = e_rho - deriv_y(twice * grad_y)

        tiles(c, work)
        if c == 0:
            start(sides(1, 0))
        if c == chunks - 1:
            start(sides(1, 1))
        for way in (0, 1):
            start(planes(1, way, c))

    def diverge(c):
        for way in (0, 1):
            planes(1, way, c).wait_recv()
        if c == chunks - 1:
            sides(1, 0).wait_recv()
        if c == 0:
            sides(1, 1).wait_recv()

        def work(at):
            span = pl.ds(at, edge)
            out[:, span, :] = out[:, span, :] - (
                deriv_z(fz[:, span, :]) + deriv_x(fx[:, pl.ds(at, 3 * edge), :])
            )

        tiles(c, work)

    gathered, done = set(), set()
    ahead = list(order) if square else []
    for c in ahead[:2]:
        relay(c)
    for i, c in enumerate(order):
        for later in ahead[2:] if i == 0 else []:
            relay(later)
        gather(c)
        gathered.add(c)
        for d in order:
            around = {e for e in (d - 1, d, d + 1) if 0 <= e < chunks}
            ends = d not in (0, chunks - 1) or {0, chunks - 1} <= gathered
            if d not in done and around <= gathered and ends and len(gathered) > 2:
                energy(d)
                done.add(d)
                break
    for d in order:
        if d not in done:
            energy(d)
    for d in order:
        diverge(d)
    for copy in started:
        copy.wait_send()


def shards(peers, slabs, states, occupations, core_density):
    nst, nz, full, deep = states.shape
    wide = full // peers
    rows = 16 if wide % 16 == 0 else 8
    chunks = wide // rows
    f32 = jnp.float32
    dma = pltpu.SemaphoreType.DMA
    return pl.pallas_call(
        functools.partial(kernel, peers, slabs, rows),
        out_shape=jax.ShapeDtypeStruct((nz, wide, deep), f32),
        in_specs=[
            pl.BlockSpec(memory_space=pl.ANY),
            pl.BlockSpec(memory_space=pltpu.SMEM),
            pl.BlockSpec(memory_space=pl.ANY),
        ],
        out_specs=pl.BlockSpec(memory_space=pltpu.VMEM),
        scratch_shapes=[
            pltpu.VMEM((peers, nst, nz, wide, deep), f32),
            pltpu.VMEM((nz, wide, deep), f32),
            pltpu.VMEM((peers - 1, nz, wide, deep), f32),
            pltpu.VMEM((peers - 1, nz, wide, deep), f32),
            pltpu.VMEM((chunks, 2, nz, rows, deep), f32),
            pltpu.VMEM((chunks, 2, nz, rows, deep), f32),
            pltpu.VMEM((nz + 4, wide + 2 * edge, deep), f32),
            pltpu.VMEM((nz + 4, wide, deep), f32),
            pltpu.VMEM((nz, wide + 2 * edge, deep), f32),
            dma((peers,)),
            dma,
            dma((peers - 1, chunks)),
            dma((peers - 1, chunks)),
            dma((chunks,)),
            dma((chunks,)),
            dma((2, 2, chunks)),
            dma((2, 2, chunks)),
            dma((2, 2)),
            dma((2, 2)),
        ],
        compiler_params=pltpu.CompilerParams(
            collective_id=0, has_side_effects=True, vmem_limit_bytes=67043328 - 640 * 1024
        ),
    )(states, occupations, core_density)


def solution(mesh):
    return jax.shard_map(
        functools.partial(shards, mesh.shape["interval"], mesh.shape["slab"]),
        mesh=mesh,
        in_specs=(P("interval", "slab", None, None), P("interval"), P("slab", None, None)),
        out_specs=P("slab", "interval", None),
        check_vma=False,
    )
```

```python
import functools
import math

import jax
import jax.numpy as jnp
from jax import lax
from jax.experimental import pallas as pl
from jax.experimental.pallas import tpu as pltpu
from jax.sharding import PartitionSpec as P

spacing = 0.25
denominator = 64.0
pbe_kappa = 0.804
pbe_mu = 0.2195149727645171
pbe_beta = 0.06672455060314922
pw_alpha = 0.0310907
pbe_gamma = (1.0 - math.log(2.0)) / math.pi**2
MESH = pl.DeviceIdType.MESH
edge = 8


def five_point(low2, low1, high1, high2):
    return (8.0 * (high1 - low1) - (high2 - low2)) * (1.0 / (12.0 * spacing))


def deriv_y(field):
    axis = field.ndim - 1
    count = field.shape[axis]
    return five_point(
        pltpu.roll(field, 2, axis),
        pltpu.roll(field, 1, axis),
        pltpu.roll(field, count - 1, axis),
        pltpu.roll(field, count - 2, axis),
    )


def deriv_x(tall):
    return five_point(
        tall[:, edge - 2 : -edge - 2],
        tall[:, edge - 1 : -edge - 1],
        tall[:, edge + 1 : 1 - edge],
        tall[:, edge + 2 : 2 - edge],
    )


def deriv_z(tall):
    count = tall.shape[0] - 4
    return five_point(
        tall[:count], tall[1 : count + 1], tall[3 : count + 3], tall[4 : count + 4]
    )


def pbe_derivs(n, g):
    k_one = (3.0 * math.pi**2) ** (1.0 / 3.0)
    ex_one = -0.75 * (3.0 / math.pi) ** (1.0 / 3.0)
    r_one = (3.0 / (4.0 * math.pi)) ** (1.0 / 3.0)
    s_one = 1.0 / (4.0 * k_one**2)
    t_one = math.pi / (16.0 * k_one)
    ratio = pbe_beta / pbe_gamma
    inv_six = jnp.exp(jnp.log(n) * (-1.0 / 6.0))
    inv = inv_six * inv_six
    inv2 = inv * inv
    inv4 = inv2 * inv2
    cube = n * inv2
    s_sq = (s_one * g) * (inv4 * inv4)
    u_inv = 1.0 / (1.0 + (pbe_mu / pbe_kappa) * s_sq)
    f_exch = (1.0 + pbe_kappa) - pbe_kappa * u_inv
    f_slope = pbe_mu * u_inv * u_inv
    ex_rho = (ex_one * cube) * ((4.0 / 3.0) * f_exch - (8.0 / 3.0) * f_slope * s_sq)

    radius = r_one * inv
    root = math.sqrt(r_one) * inv_six
    two_a = 2.0 * pw_alpha
    lower = (two_a * root) * (
        7.5957 + root * (3.5876 + root * (1.6382 + root * 0.49294))
    )
    slope = (two_a * root) * (
        0.5 * 7.5957 + root * (3.5876 + root * (1.5 * 1.6382 + root * (2.0 * 0.49294)))
    )
    pair_inv = 1.0 / (lower * (lower + 1.0))
    log_term = jnp.log(1.0 + (lower + 1.0) * pair_inv)
    front = two_a + (two_a * 0.2137) * radius
    e_corr = -front * log_term
    n_ec = (1.0 / 3.0) * ((two_a * 0.2137) * radius * log_term - front * slope * pair_inv)

    grown = jnp.exp(e_corr * (-1.0 / pbe_gamma))
    factor = ratio / (grown - 1.0)
    t_sq = (t_one * g) * (inv4 * inv2 * inv)
    y = factor * t_sq
    lift = 1.0 + y
    den = lift + y * y
    add = (ratio * t_sq) * lift
    full = den + add
    inv_full = 1.0 / (den * full)
    h_term = pbe_gamma * jnp.log(1.0 + add * (full * inv_full))
    h_t = (pbe_beta * inv_full) * (1.0 + 2.0 * y)
    h_ec = -(y * y) * (y * (2.0 + y)) * inv_full * grown
    e_rho = ex_rho + e_corr + h_term + n_ec + h_ec * n_ec - (7.0 / 3.0) * (t_sq * h_t)
    e_grad = inv4 * (t_one * h_t + (ex_one * s_one) * f_slope)
    return e_rho, e_grad


def kernel(
    peers, slabs, rows,
    states, occ, core, out,
    stage, core_v, snd, rcv, pair_out, pair_in, dens, fz, fx,
    in_sem, core_sem, rs_send, rs_recv, pair_send, pair_recv, z_send, z_recv, x_send, x_recv,
):
    nst, nz, wide = stage.shape[1], stage.shape[2], stage.shape[3]
    chunks = wide // rows
    me = lax.axis_index("interval")
    sl = lax.axis_index("slab")
    z_low = lax.rem(sl + slabs - 1, slabs)
    z_high = lax.rem(sl + 1, slabs)
    x_low = lax.rem(me + peers - 1, peers)
    x_high = lax.rem(me + 1, peers)
    square = peers == 4
    if square:
        hi, lo = lax.div(me, 2), lax.rem(me, 2)
        peer = [me, me + 1 - 2 * lo, me + 2 - 4 * hi, 3 - me]
    else:
        peer = [lax.rem(me + k, peers) for k in range(peers)]
    order = [0] + ([chunks - 1] if chunks > 1 else []) + list(range(1, chunks - 1))

    def pull(k):
        start = pl.multiple_of(peer[k] * wide, 8)
        return pltpu.make_async_copy(
            states.at[:, :, pl.ds(start, wide), :], stage.at[k], in_sem.at[k]
        )

    for k in [*range(1, peers), 0]:
        pull(k).start()
    core_copy = pltpu.make_async_copy(
        core.at[:, pl.ds(pl.multiple_of(me * wide, 8), wide), :], core_v, core_sem
    )
    core_copy.start()

    barrier = pltpu.get_barrier_semaphore()
    for k in range(1, peers):
        pl.semaphore_signal(
            barrier, inc=1, device_id=(peer[k], sl), device_id_type=MESH
        )
    for z in (z_low, z_high):
        pl.semaphore_signal(barrier, inc=1, device_id=(me, z), device_id_type=MESH)

    weights = [occ[s].astype(jnp.float32) * (1.0 / denominator) for s in range(nst)]

    def term(k, at):
        total = None
        for s in range(nst):
            value = stage[k, s, :, pl.ds(at, edge), :]
            part = (weights[s] * value) * value
            total = part if total is None else total + part
        return total

    def tiles(c, body):
        def step(t, _):
            body(pl.multiple_of(c * rows + t * edge, edge))
            return 0

        lax.fori_loop(0, rows // edge, step, 0)

    def share(k, c):
        span = pl.ds(c * rows, rows)
        return pltpu.make_async_remote_copy(
            src_ref=snd.at[k - 1, :, span, :],
            dst_ref=rcv.at[k - 1, :, span, :],
            send_sem=rs_send.at[k - 1, c],
            recv_sem=rs_recv.at[k - 1, c],
            device_id=(peer[k], sl),
            device_id_type=MESH,
        )

    def planes(field, way, c):
        ref = (dens, fz)[field]
        pad = (edge, 0)[field]
        span = pl.ds(pad + c * rows, rows)
        source, target = ((2, nz + 2), (nz, 0))[way]
        return pltpu.make_async_remote_copy(
            src_ref=ref.at[pl.ds(source, 2), span, :],
            dst_ref=ref.at[pl.ds(target, 2), span, :],
            send_sem=z_send.at[field, way, c],
            recv_sem=z_recv.at[field, way, c],
            device_id=(me, (z_low, z_high)[way]),
            device_id_type=MESH,
        )

    def sides(field, way):
        ref = (dens.at[pl.ds(2, nz)], fx)[field]
        source, target = ((edge, edge + wide), (wide, 0))[way]
        return pltpu.make_async_remote_copy(
            src_ref=ref.at[:, pl.ds(source, edge), :],
            dst_ref=ref.at[:, pl.ds(target, edge), :],
            send_sem=x_send.at[field, way],
            recv_sem=x_recv.at[field, way],
            device_id=((x_low, x_high)[way], sl),
            device_id_type=MESH,
        )

    started = []

    def start(copy):
        copy.start()
        started.append(copy)

    def near(c):
        return 1 + order.index(c) % 2

    def both(c):
        return pltpu.make_async_remote_copy(
            src_ref=pair_out.at[c],
            dst_ref=pair_in.at[c],
            send_sem=pair_send.at[c],
            recv_sem=pair_recv.at[c],
            device_id=(peer[near(c)], sl),
            device_id_type=MESH,
        )

    def relay(c):
        both(c).wait_recv()
        k = 3 - near(c)

        def fill(at):
            passed = pair_in[c, 1, :, pl.ds(pl.multiple_of(at - c * rows, edge), edge), :]
            snd[k - 1, :, pl.ds(at, edge), :] = term(k, at) + passed

        tiles(c, fill)
        start(share(k, c))

    if square:
        for k in range(1, peers):
            pull(k).wait()
        for c in order:

            def fill(at, c=c):
                here = pl.ds(pl.multiple_of(at - c * rows, edge), edge)
                pair_out[c, 0, :, here, :] = term(near(c), at)
                pair_out[c, 1, :, here, :] = term(3, at)

            tiles(c, fill)
            if c == order[0]:
                pl.semaphore_wait(barrier, peers + 1)
            if c in order[:2]:
                start(both(c))
    first = not square
    for c in [] if square else order:
        for k in range(1, peers):
            if first:
                pull(k).wait()

            def fill(at, k=k):
                snd[k - 1, :, pl.ds(at, edge), :] = term(k, at)

            tiles(c, fill)
            if first and k == 1:
                pl.semaphore_wait(barrier, peers + 1)
            start(share(k, c))
        first = False
    pull(0).wait()
    core_copy.wait()

    def gather(c):
        arrived = [3 - near(c)] if square else list(range(1, peers))
        for k in arrived:
            share(k, c).wait_recv()

        def add(at):
            total = term(0, at)
            if square:
                total = total + pair_in[c, 0, :, pl.ds(pl.multiple_of(at - c * rows, edge), edge), :]
            for k in arrived:
                total = total + rcv[k - 1, :, pl.ds(at, edge), :]
            dens[2 : nz + 2, pl.ds(at + edge, edge), :] = (
                total + core_v[:, pl.ds(at, edge), :]
            )

        tiles(c, add)
        if c == 0:
            start(sides(0, 0))
        if c == chunks - 1:
            start(sides(0, 1))
        for way in (0, 1):
            start(planes(0, way, c))

    def energy(c):
        for way in (0, 1):
            planes(0, way, c).wait_recv()
        if c == chunks - 1:
            sides(0, 0).wait_recv()
        if c == 0:
            sides(0, 1).wait_recv()

        def work(at):
            inner = pl.ds(at + edge, edge)
            n = dens[2 : nz + 2, inner, :]
            grad_z = deriv_z(dens[:, inner, :])
            grad_x = deriv_x(dens[2 : nz + 2, pl.ds(at, 3 * edge), :])
            grad_y = deriv_y(n)
            g = grad_z * grad_z + grad_x * grad_x + grad_y * grad_y
            e_rho, e_grad = pbe_derivs(n, g)
            twice = 2.0 * e_grad
            fz[2 : nz + 2, pl.ds(at, edge), :] = twice * grad_z
            fx[:, inner, :] = twice * grad_x
            out[:, pl.ds(at, edge), :] = e_rho - deriv_y(twice * grad_y)

        tiles(c, work)
        if c == 0:
            start(sides(1, 0))
        if c == chunks - 1:
            start(sides(1, 1))
        for way in (0, 1):
            start(planes(1, way, c))

    def diverge(c):
        for way in (0, 1):
            planes(1, way, c).wait_recv()
        if c == chunks - 1:
            sides(1, 0).wait_recv()
        if c == 0:
            sides(1, 1).wait_recv()

        def work(at):
            span = pl.ds(at, edge)
            out[:, span, :] = out[:, span, :] - (
                deriv_z(fz[:, span, :]) + deriv_x(fx[:, pl.ds(at, 3 * edge), :])
            )

        tiles(c, work)

    gathered, done = set(), set()
    ahead = list(order) if square else []
    for c in ahead[:2]:
        relay(c)
    for c in ahead[2:]:
        start(both(c))
    for i, c in enumerate(order):
        for later in ahead[2:] if i == 2 else []:
            relay(later)
        gather(c)
        gathered.add(c)
        for d in order:
            around = {e for e in (d - 1, d, d + 1) if 0 <= e < chunks}
            ends = d not in (0, chunks - 1) or {0, chunks - 1} <= gathered
            if d not in done and around <= gathered and ends and len(gathered) > 2:
                energy(d)
                done.add(d)
                break
    for d in order:
        if d not in done:
            energy(d)
    for d in order:
        diverge(d)
    for copy in started:
        copy.wait_send()


def shards(peers, slabs, states, occupations, core_density):
    nst, nz, full, deep = states.shape
    wide = full // peers
    rows = 16 if wide % 16 == 0 else 8
    chunks = wide // rows
    f32 = jnp.float32
    dma = pltpu.SemaphoreType.DMA
    return pl.pallas_call(
        functools.partial(kernel, peers, slabs, rows),
        out_shape=jax.ShapeDtypeStruct((nz, wide, deep), f32),
        in_specs=[
            pl.BlockSpec(memory_space=pl.ANY),
            pl.BlockSpec(memory_space=pltpu.SMEM),
            pl.BlockSpec(memory_space=pl.ANY),
        ],
        out_specs=pl.BlockSpec(memory_space=pltpu.VMEM),
        scratch_shapes=[
            pltpu.VMEM((peers, nst, nz, wide, deep), f32),
            pltpu.VMEM((nz, wide, deep), f32),
            pltpu.VMEM((peers - 1, nz, wide, deep), f32),
            pltpu.VMEM((peers - 1, nz, wide, deep), f32),
            pltpu.VMEM((chunks, 2, nz, rows, deep), f32),
            pltpu.VMEM((chunks, 2, nz, rows, deep), f32),
            pltpu.VMEM((nz + 4, wide + 2 * edge, deep), f32),
            pltpu.VMEM((nz + 4, wide, deep), f32),
            pltpu.VMEM((nz, wide + 2 * edge, deep), f32),
            dma((peers,)),
            dma,
            dma((peers - 1, chunks)),
            dma((peers - 1, chunks)),
            dma((chunks,)),
            dma((chunks,)),
            dma((2, 2, chunks)),
            dma((2, 2, chunks)),
            dma((2, 2)),
            dma((2, 2)),
        ],
        compiler_params=pltpu.CompilerParams(
            collective_id=0, has_side_effects=True, vmem_limit_bytes=67043328 - 640 * 1024
        ),
    )(states, occupations, core_density)


def solution(mesh):
    return jax.shard_map(
        functools.partial(shards, mesh.shape["interval"], mesh.shape["slab"]),
        mesh=mesh,
        in_specs=(P("interval", "slab", None, None), P("interval"), P("slab", None, None)),
        out_specs=P("slab", "interval", None),
        check_vma=False,
    )
```
